32 devices in a mesh: section: 4 (over y, x), tile: 8 (over z, core).
Axes of the slice: x: 2, y: 2, z: 4, core: 2. Of those that a mesh axis runs over, the one named last changes fastest.
Arguments:
- stored_inputs: bfloat16 [4, 4, 24, 128, 1024], P('section', None, 'tile'), may hold values from -6 to 6
- cotangent: bfloat16 [4, 24, 128, 1024], P(None, 'tile'), may hold values from -6 to 6
- w_reduce: bfloat16 [4, 1024, 256], P('section'), may hold values from -0.1875 to 0.1875
- w_spatial: bfloat16 [4, 2304, 256], P('section'), may hold values from -0.125 to 0.125
- w_expand: bfloat16 [4, 256, 1024], P('section'), may hold values from -0.375 to 0.375
- bias_reduce: float32 [4, 256], P('section'), may hold values from -1 to 1
- bias_spatial: float32 [4, 256], P('section'), may hold values from -1 to 1
- bias_expand: float32 [4, 1024], P('section'), may hold values from 0.5 to 2
Outputs:
- input_grads: bfloat16 [4, 4, 24, 128, 1024], P('section', None, 'tile')
- grad_reduce: float32 [4, 1024, 256], P('section', 'tile')
- grad_spatial: float32 [4, 2304, 256], P('section', 'tile')
- grad_expand: float32 [4, 256, 1024], P('section', 'tile')
The draws below stay inside these ranges and needn't reach their ends.
All inputs are finite; a program needn't handle non-finite values.
Results may differ from the reference program's by a relative error of at most 0.024.
Values may be sent and summed in bfloat16 or wider, within the bound.
A program may use at most 64 MiB of HBM per device.

```python
import jax
import jax.numpy as jnp
from jax import lax

D = 1024
B = 256
COLS = 128
MICRO = 4
SECTIONS = 4
HEIGHT = 24


def block_scale(stream_key, shape, cuts, low, high):
    def one(position, blocks):
        draws = jax.random.uniform(jax.random.fold_in(jax.random.fold_in(stream_key, 6), position), (blocks,), jnp.float32, low / len(cuts), high / len(cuts))
        return jnp.repeat(jnp.exp(draws), shape[position] // blocks).reshape((-1,) + (1,) * (len(shape) - position - 1))

    gain = one(*cuts[0])
    for cut in cuts[1:]:
        gain = gain * one(*cut)
    return gain


def normal_values(key, extent, scale, bound, shards=(), dtype=jnp.bfloat16):
    gain = block_scale(key, extent, shards, -0.22, 0.18) if shards else 1.0
    array = jax.random.normal(key, extent, jnp.float32) * scale * gain
    return jnp.minimum(jnp.maximum(array, -bound), bound).astype(dtype)


def setup_inputs(seed: int = 0) -> dict:
    seeds = jax.random.split(jax.random.key(seed), 9)
    return {
        "stored_inputs": normal_values(seeds[0], (SECTIONS, MICRO, HEIGHT, COLS, D), 1.0, 6.0, ((0, 4), (2, 8))),
        "cotangent": normal_values(seeds[1], (MICRO, HEIGHT, COLS, D), 1.0, 6.0, ((1, 8),)),
        "w_reduce": normal_values(seeds[2], (SECTIONS, D, B), D ** -0.5, 0.1875, ((0, 4),)),
        "w_spatial": normal_values(seeds[3], (SECTIONS, 9 * B, B), (9 * B) ** -0.5, 0.125, ((0, 4),)),
        "w_expand": normal_values(seeds[4], (SECTIONS, B, D), B ** -0.5, 0.375, ((0, 4),)),
        "bias_reduce": jnp.clip(jax.random.uniform(seeds[5], (SECTIONS, B), jnp.float32, -1.0, 1.0) * block_scale(seeds[5], (SECTIONS, B), ((0, 4),), -0.4, 0.0), -1.0, 1.0),
        "bias_spatial": jnp.clip(jax.random.uniform(seeds[6], (SECTIONS, B), jnp.float32, -1.0, 1.0) * block_scale(seeds[6], (SECTIONS, B), ((0, 4),), -0.4, 0.0), -1.0, 1.0),
        "bias_expand": jnp.clip(0.5 + 1.5 * jax.random.uniform(seeds[7], (SECTIONS, D), jnp.float32) ** block_scale(seeds[7], (SECTIONS, D), ((0, 4),), -0.2, 0.2), 0.5, 2.0),
    }


def silu_slope(pre_act):
    sigma_val = jax.nn.sigmoid(pre_act)
    return sigma_val * (1.0 + pre_act * (1.0 - sigma_val))


def tap_views(padded, flip_sign):
    row_count = padded.shape[-3] - 2
    col_count = padded.shape[-2]
    widened = jnp.pad(padded, [(0, 0)] * (padded.ndim - 2) + [(1, 1), (0, 0)])
    pieces_list = []
    for row_off in (-1, 0, 1):
        for col_off in (-1, 0, 1):
            row_start = 1 + flip_sign * row_off
            col_start = 1 + flip_sign * col_off
            window = lax.slice_in_dim(widened, row_start, row_start + row_count, axis=widened.ndim - 3)
            window = lax.slice_in_dim(window, col_start, col_start + col_count, axis=widened.ndim - 2)
            pieces_list.append(window)
    return jnp.concatenate(pieces_list, axis=-1)


def contract_rows(left_mat, right_mat):
    return lax.dot_general(left_mat, right_mat, (((0,), (0,)), ((), ())), preferred_element_type=jnp.float32)


def contract_cols(left_mat, right_mat):
    return lax.dot_general(left_mat, right_mat, (((1,), (1,)), ((), ())), preferred_element_type=jnp.float32)


def reference(stored_inputs, cotangent, w_reduce, w_spatial, w_expand, bias_reduce, bias_spatial, bias_expand):
    section_count, micro_count, height, width_px, model_w = stored_inputs.shape
    bottle = w_reduce.shape[2]
    pixels = height * width_px
    sums_one = [jnp.zeros((model_w, bottle), jnp.float32) for section_id in range(section_count)]
    sums_two = [jnp.zeros((9 * bottle, bottle), jnp.float32) for section_id in range(section_count)]
    sums_three = [jnp.zeros((bottle, model_w), jnp.float32) for section_id in range(section_count)]
    results = [[None] * micro_count for section_id in range(section_count)]
    for micro_id in range(micro_count):
        upstream = cotangent[micro_id]
        for section_id in range(section_count - 1, -1, -1):
            flat_in = stored_inputs[section_id, micro_id].reshape(pixels, model_w)
            pre_one = jnp.dot(flat_in, w_reduce[section_id], preferred_element_type=jnp.float32) + bias_reduce[section_id]
            act_one = jax.nn.silu(pre_one).astype(jnp.bfloat16)
            padded = jnp.pad(act_one.reshape(height, width_px, bottle), ((1, 1), (0, 0), (0, 0)))
            patches = tap_views(padded, 1).reshape(pixels, 9 * bottle)
            pre_two = jnp.dot(patches, w_spatial[section_id], preferred_element_type=jnp.float32) + bias_spatial[section_id]
            act_two = jax.nn.silu(pre_two).astype(jnp.bfloat16)
            pre_three = jnp.dot(act_two, w_expand[section_id], preferred_element_type=jnp.float32) + bias_expand[section_id] + flat_in.astype(jnp.float32)
            slope_three = upstream.reshape(pixels, model_w).astype(jnp.float32) * silu_slope(pre_three)
            grad_three = slope_three.astype(jnp.bfloat16)
            sums_three[section_id] = sums_three[section_id] + contract_rows(act_two, grad_three)
            grad_two = (contract_cols(grad_three, w_expand[section_id]) * silu_slope(pre_two)).astype(jnp.bfloat16)
            sums_two[section_id] = sums_two[section_id] + contract_rows(patches, grad_two)
            grad_pad = jnp.pad(grad_two.reshape(height, width_px, bottle), ((1, 1), (0, 0), (0, 0)))
            back_patches = tap_views(grad_pad, -1).reshape(pixels, 9 * bottle)
            w_turned = w_spatial[section_id].reshape(9, bottle, bottle).transpose(0, 2, 1).reshape(9 * bottle, bottle)
            spatial_back = jnp.dot(back_patches, w_turned, preferred_element_type=jnp.float32)
            grad_one = (spatial_back * silu_slope(pre_one)).astype(jnp.bfloat16)
            sums_one[section_id] = sums_one[section_id] + contract_rows(flat_in, grad_one)
            input_grad = (contract_cols(grad_one, w_reduce[section_id]) + slope_three).astype(jnp.bfloat16)
            upstream = input_grad.reshape(height, width_px, model_w)
            results[section_id][micro_id] = upstream
    input_grads = jnp.stack([jnp.stack(results[section_id]) for section_id in range(section_count)])
    return input_grads, jnp.stack(sums_one), jnp.stack(sums_two), jnp.stack(sums_three)
```

```python
import functools

import jax
import jax.numpy as jnp
from jax import lax
from jax.experimental import pallas as pl
from jax.experimental.pallas import tpu as pltpu
from jax.sharding import PartitionSpec as P

BF = jnp.bfloat16
F32 = jnp.float32
PAD = 8
PIECES = 4


def silu_and_slope(pre_act):
    sigma_val = jax.nn.sigmoid(pre_act)
    return pre_act * sigma_val, sigma_val * (1.0 + pre_act * (1.0 - sigma_val))


def dot_nn(left, right):
    return jnp.dot(left, right, preferred_element_type=F32)


def dot_nt(left, right):
    return lax.dot_general(left, right, (((1,), (1,)), ((), ())), preferred_element_type=F32)


def dot_tn(left, right):
    return lax.dot_general(left, right, (((0,), (0,)), ((), ())), preferred_element_type=F32)


def kernel(
    sections, tiles, x_ref, cot_ref, w1_ref, w2_ref, w3_ref, b1_ref, b2_ref, b3_ref,
    gin_ref, o1_ref, o2_ref, o3_ref,
    up, slope1, slope2, slope3, act_pad, taps, act2, g_pad, g3, g1,
    fe_out, fe_in, be_out, be_in, sum1, sum2, sum3,
    p1, p2, p3, q1, q2, q3, r1, r2, r3, s1, s2, s3,
    cot_sem, up_ss, up_rs, fe_ss, fe_rs, be_ss, be_rs, a_ss, a_rs, z_ss, z_rs,
):
    micros, rows, cols, model = x_ref.shape
    bottle = w1_ref.shape[1]
    pixels = rows * cols
    width = cols // PIECES
    half = tiles // 2
    sec = lax.axis_index("section")
    tile = lax.axis_index("tile")
    core = lax.rem(tile, 2)
    zed = tile // 2
    is_last = sec == sections - 1
    has_above = tile > 0
    has_below = tile < tiles - 1
    partner = tile + 1 - 2 * core

    barrier = pltpu.get_barrier_semaphore()

    def greet(cond, target):
        @pl.when(cond)
        def _():
            pl.semaphore_signal(barrier, inc=1, device_id=target, device_id_type=pl.DeviceIdType.MESH)

    greet(has_above, {"tile": tile - 1})
    greet(has_below, {"tile": tile + 1})
    greet(sec > 0, {"section": sec - 1})
    greet(sec < sections - 1, {"section": sec + 1})
    for step in range(1, half):
        other = lax.rem(zed + step, half) * 2 + core
        pl.semaphore_signal(barrier, inc=1, device_id={"tile": other}, device_id_type=pl.DeviceIdType.MESH)

    def cot_copy(m):
        return pltpu.make_async_copy(cot_ref.at[m], up.at[m], cot_sem.at[m])

    @pl.when(is_last)
    def _():
        for m in range(micros):
            cot_copy(m).start()

    act_pad[...] = jnp.zeros(act_pad.shape, F32)
    g_pad[...] = jnp.zeros(g_pad.shape, F32)
    sum1[...] = jnp.zeros(sum1.shape, F32)
    sum2[...] = jnp.zeros(sum2.shape, F32)
    sum3[...] = jnp.zeros(sum3.shape, F32)

    def remote(src, dst, ss, rs, target):
        return pltpu.make_async_remote_copy(
            src_ref=src, dst_ref=dst, send_sem=ss, recv_sem=rs,
            device_id=target, device_id_type=pl.DeviceIdType.MESH,
        )

    def fe_up(m):
        return remote(fe_out.at[m, 0], fe_in.at[m, 1], fe_ss.at[m, 0], fe_rs.at[m, 1], {"tile": tile - 1})

    def fe_down(m):
        return remote(fe_out.at[m, 1], fe_in.at[m, 0], fe_ss.at[m, 1], fe_rs.at[m, 0], {"tile": tile + 1})

    def cut(j):
        return pl.ds(j * width, width)

    def be_up(m, j):
        n = m * PIECES + j
        return remote(
            be_out.at[m, 0, cut(j)], be_in.at[m, 1, cut(j)], be_ss.at[n, 0], be_rs.at[n, 1],
            {"tile": tile - 1},
        )

    def be_down(m, j):
        n = m * PIECES + j
        return remote(
            be_out.at[m, 1, cut(j)], be_in.at[m, 0, cut(j)], be_ss.at[n, 1], be_rs.at[n, 0],
            {"tile": tile + 1},
        )

    def relay(m, j):
        n = m * PIECES + j
        return remote(
            gin_ref.at[m, :, cut(j)], up.at[m, :, cut(j)], up_ss.at[n], up_rs.at[n],
            {"section": sec - 1},
        )

    def reduce_in(m, _):
        for y in range(rows):
            pre = dot_nn(x_ref[m, y], w1_ref[...]) + b1_ref[...]
            act, slope = silu_and_slope(pre)
            slope1[m, y] = slope
            act = act.astype(BF)
            act_pad[m, y + 1, pl.ds(PAD, cols)] = act.astype(F32)
            if y == 0:
                fe_out[m, 0] = act
            if y == rows - 1:
                fe_out[m, 1] = act
        return 0

    lax.fori_loop(0, micros, reduce_in, 0)

    greetings = (
        has_above.astype(jnp.int32) + has_below.astype(jnp.int32) + (sec > 0).astype(jnp.int32)
        + (sec < sections - 1).astype(jnp.int32) + (half - 1)
    )
    pl.semaphore_wait(barrier, greetings)

    @pl.when(has_above)
    def _():
        for m in range(micros):
            fe_up(m).start()

    @pl.when(has_below)
    def _():
        for m in range(micros):
            fe_down(m).start()

    def expand_out(m, _):
        @pl.when(has_above)
        def _():
            fe_down(m).wait_recv()
            act_pad[m, 0, pl.ds(PAD, cols)] = fe_in[m, 0].astype(F32)

        @pl.when(has_below)
        def _():
            fe_up(m).wait_recv()
            act_pad[m, rows + 1, pl.ds(PAD, cols)] = fe_in[m, 1].astype(F32)

        for shift in range(3):
            for y in range(rows + 2):
                taps[shift, m, y] = act_pad[m, y, pl.ds(PAD - 1 + shift, cols)].astype(BF)
        for y in range(rows):
            patch = jnp.concatenate(
                [taps[dx, m, y + dy] for dy in range(3) for dx in range(3)], axis=-1
            )
            pre = dot_nn(patch, w2_ref[...]) + b2_ref[...]
            act, slope = silu_and_slope(pre)
            slope2[m, y] = slope
            act = act.astype(BF)
            act2[m, y] = act
            for n in range(model // bottle):
                lanes = pl.ds(n * bottle, bottle)
                pre = dot_nn(act, w3_ref[:, lanes]) + b3_ref[:, lanes] + x_ref[m, y, :, lanes].astype(F32)
                slope3[m, y, :, lanes] = silu_and_slope(pre)[1]
        return 0

    lax.fori_loop(0, micros, expand_out, 0)

    def outer_part(m, j):
        @pl.when(jnp.logical_not(is_last))
        def _():
            relay(m, j).wait_recv()

        for y in range(rows):
            g3[y, cut(j)] = (up[m, y, cut(j)].astype(F32) * slope3[m, y, cut(j)]).astype(BF)
        back = dot_nt(g3[:, cut(j)].reshape(rows * width, model), w3_ref[...])
        g2 = (back.reshape(rows, width, bottle) * slope2[m, :, cut(j)]).astype(BF)
        g_pad[m, pl.ds(1, rows), pl.ds(PAD + j * width, width)] = g2.astype(F32)
        be_out[m, 0, cut(j)] = g2[0]
        be_out[m, 1, cut(j)] = g2[rows - 1]

        @pl.when(has_above)
        def _():
            be_up(m, j).start()

        @pl.when(has_below)
        def _():
            be_down(m, j).start()

    def take_rims(m, j):
        @pl.when(has_above)
        def _():
            be_down(m, j).wait_recv()
            g_pad[m, 0, pl.ds(PAD + j * width, width)] = be_in[m, 0, cut(j)].astype(F32)

        @pl.when(has_below)
        def _():
            be_up(m, j).wait_recv()
            g_pad[m, rows + 1, pl.ds(PAD + j * width, width)] = be_in[m, 1, cut(j)].astype(F32)

    def inner_part(m, j):
        total = jnp.zeros((rows * width, bottle), F32)
        for dx in range(3):
            moved = g_pad[m, :, pl.ds(PAD + 1 + j * width - dx, width)].astype(BF)
            for dy in range(3):
                piece = moved[2 - dy : 2 - dy + rows].reshape(rows * width, bottle)
                total = total + dot_nt(piece, w2_ref[pl.ds((3 * dy + dx) * bottle, bottle)])
        grad = (total.reshape(rows, width, bottle) * slope1[m, :, cut(j)]).astype(BF)
        g1[:, cut(j)] = grad
        for y in range(rows):
            direct = up[m, y, cut(j)].astype(F32) * slope3[m, y, cut(j)]
            gin_ref[m, y, cut(j)] = (dot_nt(grad[y], w1_ref[...]) + direct).astype(BF)

        @pl.when(sec > 0)
        def _():
            relay(m, j).start()

    def backward(m, _):
        @pl.when(is_last)
        def _():
            cot_copy(m).wait()

        outer_part(m, 0)
        take_rims(m, 0)
        for j in range(1, PIECES):
            outer_part(m, j)
            take_rims(m, j)
            inner_part(m, j - 1)
        inner_part(m, PIECES - 1)
        sum3[...] += dot_tn(act2[m].reshape(pixels, bottle), g3[...].reshape(pixels, model))
        g2 = g_pad[m, pl.ds(1, rows), pl.ds(PAD, cols)].astype(BF).reshape(pixels, bottle)
        for dy in range(3):
            for dx in range(3):
                patch = taps[dx, m, pl.ds(dy, rows)].reshape(pixels, bottle)
                sum2[pl.ds((3 * dy + dx) * bottle, bottle)] += dot_tn(patch, g2)
        sum1[...] += dot_tn(x_ref[m].reshape(pixels, model), g1[...].reshape(pixels, bottle))
        return 0

    lax.fori_loop(0, micros, backward, 0)

    kinds = (
        (sum3, p3, q3, r3, s3, o3_ref),
        (sum2, p2, q2, r2, s2, o2_ref),
        (sum1, p1, q1, r1, s1, o1_ref),
    )

    def swap(kind):
        total, sent, got, _, _, _ = kinds[kind]
        return remote(sent, got, a_ss.at[kind], a_rs.at[kind], {"tile": partner})

    def spread(kind, step):
        _, _, _, part, landed, _ = kinds[kind]
        there = lax.rem(zed + step, half)
        n = kind * half + step
        return remote(
            part.at[there], landed.at[step - 1], z_ss.at[n], z_rs.at[n], {"tile": there * 2 + core}
        )

    for kind, (total, sent, _, _, _, out) in enumerate(kinds):
        span = out.shape[0]
        for z in range(half):
            first = pl.multiple_of((2 * z + 1 - core) * span, 16)
            sent[z] = total[pl.ds(first, span)].astype(BF)
        swap(kind).start()
    for kind, (total, _, got, part, _, out) in enumerate(kinds):
        span = out.shape[0]
        swap(kind).wait_recv()
        for z in range(half):
            first = pl.multiple_of((2 * z + core) * span, 16)
            part[z] = (total[pl.ds(first, span)] + got[z].astype(F32)).astype(BF)
        for step in range(1, half):
            spread(kind, step).start()
        own = pl.multiple_of((2 * zed + core) * span, 16)
        out[...] = total[pl.ds(own, span)] + got[zed].astype(F32)
    for kind, (_, _, _, _, landed, out) in enumerate(kinds):
        value = out[...]
        for step in range(1, half):
            spread(kind, step).wait_recv()
            value = value + landed[step - 1].astype(F32)
        out[...] = value

    def close(m, _):
        @pl.when(has_above)
        def _():
            fe_up(m).wait_send()
            for j in range(PIECES):
                be_up(m, j).wait_send()

        @pl.when(has_below)
        def _():
            fe_down(m).wait_send()
            for j in range(PIECES):
                be_down(m, j).wait_send()

        @pl.when(sec > 0)
        def _():
            for j in range(PIECES):
                relay(m, j).wait_send()

        return 0

    lax.fori_loop(0, micros, close, 0)
    for kind in range(3):
        swap(kind).wait_send()
        for step in range(1, half):
            spread(kind, step).wait_send()


def local(
    sections, tiles,
    stored_inputs, cotangent, w_reduce, w_spatial, w_expand, bias_reduce, bias_spatial, bias_expand,
):
    _, micros, rows, cols, model = stored_inputs.shape
    bottle = w_reduce.shape[2]
    half = tiles // 2
    spans = (model // tiles, 9 * bottle // tiles, bottle // tiles)
    wides = (bottle, bottle, model)
    vmem = pltpu.VMEM
    dma = pltpu.SemaphoreType.DMA
    whole = pl.BlockSpec(memory_space=pltpu.VMEM)
    scratch = [
        vmem((micros, rows, cols, model), BF),
        vmem((micros, rows, cols, bottle), F32),
        vmem((micros, rows, cols, bottle), F32),
        vmem((micros, rows, cols, model), F32),
        vmem((micros, rows + 2, cols + 2 * PAD, bottle), F32),
        vmem((3, micros, rows + 2, cols, bottle), BF),
        vmem((micros, rows, cols, bottle), BF),
        vmem((micros, rows + 2, cols + 2 * PAD, bottle), F32),
        vmem((rows, cols, model), BF),
        vmem((rows, cols, bottle), BF),
    ]
    scratch += [vmem((micros, 2, cols, bottle), BF)] * 4
    scratch += [vmem((span * tiles, wide), F32) for span, wide in zip(spans, wides)]
    for count in (half, half, half, half - 1):
        scratch += [vmem((count, span, wide), BF) for span, wide in zip(spans, wides)]
    pieces = micros * PIECES
    scratch += [
        dma((micros,)), dma((pieces,)), dma((pieces,)), dma((micros, 2)), dma((micros, 2)),
        dma((pieces, 2)), dma((pieces, 2)), dma((3,)), dma((3,)), dma((3 * half,)), dma((3 * half,)),
    ]
    outs = pl.pallas_call(
        functools.partial(kernel, sections, tiles),
        out_shape=[jax.ShapeDtypeStruct((micros, rows, cols, model), BF)]
        + [jax.ShapeDtypeStruct((span, wide), F32) for span, wide in zip(spans, wides)],
        in_specs=[whole, pl.BlockSpec(memory_space=pl.ANY)] + [whole] * 6,
        out_specs=[whole] * 4,
        scratch_shapes=scratch,
        compiler_params=pltpu.CompilerParams(
            collective_id=0, has_side_effects=True, vmem_limit_bytes=66 * 1024 * 1000
        ),
    )(
        stored_inputs[0], cotangent, w_reduce[0], w_spatial[0], w_expand[0],
        bias_reduce, bias_spatial, bias_expand,
    )
    return tuple(out[None] for out in outs)


def solution(mesh):
    return jax.shard_map(
        functools.partial(local, mesh.shape["section"], mesh.shape["tile"]),
        mesh=mesh,
        in_specs=(
            P("section", None, "tile", None, None),
            P(None, "tile", None, None),
            P("section", None, None),
            P("section", None, None),
            P("section", None, None),
            P("section", None),
            P("section", None),
            P("section", None),
        ),
        out_specs=(
            P("section", None, "tile", None, None),
            P("section", "tile", None),
            P("section", "tile", None),
            P("section", "tile", None),
        ),
        check_vma=False,
    )
```

```python
import functools

import jax
import jax.numpy as jnp
from jax import lax
from jax.experimental import pallas as pl
from jax.experimental.pallas import tpu as pltpu
from jax.sharding import PartitionSpec as P

BF = jnp.bfloat16
F32 = jnp.float32
PAD = 8
PIECES = 8
LAG = 2


def silu_and_slope(pre_act):
    sigma_val = jax.nn.sigmoid(pre_act)
    return pre_act * sigma_val, sigma_val * (1.0 + pre_act * (1.0 - sigma_val))


def dot_nn(left, right):
    return jnp.dot(left, right, preferred_element_type=F32)


def dot_tn(left, right):
    return lax.dot_general(left, right, (((0,), (0,)), ((), ())), preferred_element_type=F32)


def kernel(
    sections, tiles, x_ref, cot_ref, w1_ref, w2_ref, w3_ref, b1_ref, b2_ref, b3_ref,
    gin_ref, o1_ref, o2_ref, o3_ref,
    up, slope1, slope2, slope3, act_pad, taps, act2, g_pad, g3, g1,
    t1, t2, t3, fe_out, fe_in, be_out, be_in, sum1, sum2, sum3,
    p1, p2, p3, q1, q2, q3, r1, r2, r3, s1, s2, s3,
    cot_sem, up_ss, up_rs, fe_ss, fe_rs, be_ss, be_rs, a_ss, a_rs, z_ss, z_rs,
):
    micros, rows, cols, model = x_ref.shape
    bottle = w1_ref.shape[1]
    pixels = rows * cols
    width = cols // PIECES
    half = tiles // 2
    sec = lax.axis_index("section")
    tile = lax.axis_index("tile")
    core = lax.rem(tile, 2)
    zed = tile // 2
    is_last = sec == sections - 1
    has_above = tile > 0
    has_below = tile < tiles - 1
    partner = tile + 1 - 2 * core

    barrier = pltpu.get_barrier_semaphore()

    def greet(cond, target):
        @pl.when(cond)
        def _():
            pl.semaphore_signal(barrier, inc=1, device_id=target, device_id_type=pl.DeviceIdType.MESH)

    greet(has_above, {"tile": tile - 1})
    greet(has_below, {"tile": tile + 1})
    greet(sec > 0, {"section": sec - 1})
    greet(sec < sections - 1, {"section": sec + 1})
    for step in range(1, half):
        other = lax.rem(zed + step, half) * 2 + core
        pl.semaphore_signal(barrier, inc=1, device_id={"tile": other}, device_id_type=pl.DeviceIdType.MESH)

    def cot_copy(m):
        return pltpu.make_async_copy(cot_ref.at[m], up.at[m], cot_sem.at[m])

    @pl.when(is_last)
    def _():
        for m in range(micros):
            cot_copy(m).start()

    act_pad[...] = jnp.zeros(act_pad.shape, F32)
    g_pad[...] = jnp.zeros(g_pad.shape, F32)
    sum1[...] = jnp.zeros(sum1.shape, F32)
    sum2[...] = jnp.zeros(sum2.shape, F32)
    sum3[...] = jnp.zeros(sum3.shape, F32)

    def remote(src, dst, ss, rs, target):
        return pltpu.make_async_remote_copy(
            src_ref=src, dst_ref=dst, send_sem=ss, recv_sem=rs,
            device_id=target, device_id_type=pl.DeviceIdType.MESH,
        )

    def fe_up(m):
        return remote(fe_out.at[m, 0], fe_in.at[m, 1], fe_ss.at[m, 0], fe_rs.at[m, 1], {"tile": tile - 1})

    def fe_down(m):
        return remote(fe_out.at[m, 1], fe_in.at[m, 0], fe_ss.at[m, 1], fe_rs.at[m, 0], {"tile": tile + 1})

    def cut(j):
        return pl.ds(j * width, width)

    def be_up(m, j):
        n = m * PIECES + j
        return remote(
            be_out.at[m, 0, cut(j)], be_in.at[m, 1, cut(j)], be_ss.at[n, 0], be_rs.at[n, 1],
            {"tile": tile - 1},
        )

    def be_down(m, j):
        n = m * PIECES + j
        return remote(
            be_out.at[m, 1, cut(j)], be_in.at[m, 0, cut(j)], be_ss.at[n, 1], be_rs.at[n, 0],
            {"tile": tile + 1},
        )

    def relay(m, j):
        n = m * PIECES + j
        return remote(
            gin_ref.at[m, :, cut(j)], up.at[m, :, cut(j)], up_ss.at[n], up_rs.at[n],
            {"section": sec - 1},
        )

    def reduce_in(m, _):
        for y in range(rows):
            pre = dot_nn(x_ref[m, y], w1_ref[...]) + b1_ref[...]
            act, slope = silu_and_slope(pre)
            slope1[m, y] = slope
            act = act.astype(BF)
            act_pad[m, y + 1, pl.ds(PAD, cols)] = act.astype(F32)
            if y == 0:
                fe_out[m, 0] = act
            if y == rows - 1:
                fe_out[m, 1] = act
        return 0

    reduce_in(0, 0)

    greetings = (
        has_above.astype(jnp.int32) + has_below.astype(jnp.int32) + (sec > 0).astype(jnp.int32)
        + (sec < sections - 1).astype(jnp.int32) + (half - 1)
    )
    pl.semaphore_wait(barrier, greetings)

    def share_rims(m):
        @pl.when(has_above)
        def _():
            fe_up(m).start()

        @pl.when(has_below)
        def _():
            fe_down(m).start()

    def reduce_and_share(m, _):
        reduce_in(m, 0)
        share_rims(m)
        return 0

    share_rims(0)
    for n in range(model // bottle):
        lanes = pl.ds(n * bottle, bottle)
        t1[:, lanes] = w1_ref[lanes, :].astype(F32).T.astype(BF)
        t3[lanes, :] = w3_ref[:, lanes].astype(F32).T.astype(BF)
    for n in range(9):
        band = pl.ds(n * bottle, bottle)
        t2[band, :] = w2_ref[band, :].astype(F32).T.astype(BF)
    lax.fori_loop(1, micros, reduce_and_share, 0)

    def expand_out(m, _):
        @pl.when(has_above)
        def _():
            fe_down(m).wait_recv()
            act_pad[m, 0, pl.ds(PAD, cols)] = fe_in[m, 0].astype(F32)

        @pl.when(has_below)
        def _():
            fe_up(m).wait_recv()
            act_pad[m, rows + 1, pl.ds(PAD, cols)] = fe_in[m, 1].astype(F32)

        for shift in range(3):
            for y in range(rows + 2):
                taps[shift, m, y] = act_pad[m, y, pl.ds(PAD - 1 + shift, cols)].astype(BF)
        for y in range(rows):
            patch = jnp.concatenate(
                [taps[dx, m, y + dy] for dy in range(3) for dx in range(3)], axis=-1
            )
            pre = dot_nn(patch, w2_ref[...]) + b2_ref[...]
            act, slope = silu_and_slope(pre)
            slope2[m, y] = slope
            act = act.astype(BF)
            act2[m, y] = act
            for n in range(model // bottle):
                lanes = pl.ds(n * bottle, bottle)
                pre = dot_nn(act, w3_ref[:, lanes]) + b3_ref[:, lanes] + x_ref[m, y, :, lanes].astype(F32)
                slope3[m, y, :, lanes] = silu_and_slope(pre)[1]
        return 0

    @pl.when(jnp.logical_not(is_last))
    def _():
        lax.fori_loop(0, micros, expand_out, 0)

    def outer_part(m, j):
        @pl.when(jnp.logical_not(is_last))
        def _():
            relay(m, j).wait_recv()

        for y in range(rows):
            g3[y, cut(j)] = (up[m, y, cut(j)].astype(F32) * slope3[m, y, cut(j)]).astype(BF)
        back = dot_nn(g3[:, cut(j)].reshape(rows * width, model), t3[...])
        g2 = (back.reshape(rows, width, bottle) * slope2[m, :, cut(j)]).astype(BF)
        g_pad[m, pl.ds(1, rows), pl.ds(PAD + j * width, width)] = g2.astype(F32)
        be_out[m, 0, cut(j)] = g2[0]
        be_out[m, 1, cut(j)] = g2[rows - 1]

        @pl.when(has_above)
        def _():
            be_up(m, j).start()

        @pl.when(has_below)
        def _():
            be_down(m, j).start()

    def take_rims(m, j):
        @pl.when(has_above)
        def _():
            be_down(m, j).wait_recv()
            g_pad[m, 0, pl.ds(PAD + j * width, width)] = be_in[m, 0, cut(j)].astype(F32)

        @pl.when(has_below)
        def _():
            be_up(m, j).wait_recv()
            g_pad[m, rows + 1, pl.ds(PAD + j * width, width)] = be_in[m, 1, cut(j)].astype(F32)

    def inner_part(m, j):
        moved = [
            g_pad[m, :, pl.ds(PAD + 1 + j * width - dx, width)].astype(BF) for dx in range(3)
        ]
        patch = jnp.concatenate(
            [
                moved[dx][2 - dy : 2 - dy + rows].reshape(rows * width, bottle)
                for dy in range(3)
                for dx in range(3)
            ],
            axis=-1,
        )
        total = dot_nn(patch, t2[...])
        grad = (total.reshape(rows, width, bottle) * slope1[m, :, cut(j)]).astype(BF)
        g1[:, cut(j)] = grad
        flat = grad.reshape(rows * width, bottle)
        for n in range(model // bottle):
            lanes = pl.ds(n * bottle, bottle)
            back = dot_nn(flat, t1[:, lanes]).reshape(rows, width, bottle)
            direct = up[m, :, cut(j), lanes].astype(F32) * slope3[m, :, cut(j), lanes]
            gin_ref[m, :, cut(j), lanes] = (back + direct).astype(BF)

        @pl.when(sec > 0)
        def _():
            relay(m, j).start()

    def backward(m, _):
        @pl.when(is_last)
        def _():
            expand_out(m, 0)
            cot_copy(m).wait()

        for j in range(PIECES):
            outer_part(m, j)
            if j >= LAG:
                take_rims(m, j - LAG)
            if j > LAG:
                inner_part(m, j - LAG - 1)
        for j in range(PIECES - LAG, PIECES):
            take_rims(m, j)
            inner_part(m, j - 1)
        inner_part(m, PIECES - 1)
        sum3[...] += dot_tn(act2[m].reshape(pixels, bottle), g3[...].reshape(pixels, model))
        g2 = g_pad[m, pl.ds(1, rows), pl.ds(PAD, cols)].astype(BF).reshape(pixels, bottle)
        for dy in range(3):
            for dx in range(3):
                patch = taps[dx, m, pl.ds(dy, rows)].reshape(pixels, bottle)
                sum2[pl.ds((3 * dy + dx) * bottle, bottle)] += dot_tn(patch, g2)
        sum1[...] += dot_tn(x_ref[m].reshape(pixels, model), g1[...].reshape(pixels, bottle))
        return 0

    lax.fori_loop(0, micros, backward, 0)

    kinds = (
        (sum3, p3, q3, r3, s3, o3_ref),
        (sum2, p2, q2, r2, s2, o2_ref),
        (sum1, p1, q1, r1, s1, o1_ref),
    )

    def swap(kind):
        total, sent, got, _, _, _ = kinds[kind]
        return remote(sent, got, a_ss.at[kind], a_rs.at[kind], {"tile": partner})

    def spread(kind, step):
        _, _, _, part, landed, _ = kinds[kind]
        there = lax.rem(zed + step, half)
        n = kind * half + step
        return remote(
            part.at[there], landed.at[step - 1], z_ss.at[n], z_rs.at[n], {"tile": there * 2 + core}
        )

    for kind, (total, sent, _, _, _, out) in enumerate(kinds):
        span = out.shape[0]
        for z in range(half):
            first = pl.multiple_of((2 * z + 1 - core) * span, 16)
            sent[z] = total[pl.ds(first, span)].astype(BF)
        swap(kind).start()
    for kind, (total, _, got, part, _, out) in enumerate(kinds):
        span = out.shape[0]
        swap(kind).wait_recv()
        for z in range(half):
            first = pl.multiple_of((2 * z + core) * span, 16)
            part[z] = (total[pl.ds(first, span)] + got[z].astype(F32)).astype(BF)
        for step in range(1, half):
            spread(kind, step).start()
        own = pl.multiple_of((2 * zed + core) * span, 16)
        out[...] = total[pl.ds(own, span)] + got[zed].astype(F32)
    for kind, (_, _, _, _, landed, out) in enumerate(kinds):
        value = out[...]
        for step in range(1, half):
            spread(kind, step).wait_recv()
            value = value + landed[step - 1].astype(F32)
        out[...] = value

    def close(m, _):
        @pl.when(has_above)
        def _():
            fe_up(m).wait_send()
            for j in range(PIECES):
                be_up(m, j).wait_send()

        @pl.when(has_below)
        def _():
            fe_down(m).wait_send()
            for j in range(PIECES):
                be_down(m, j).wait_send()

        @pl.when(sec > 0)
        def _():
            for j in range(PIECES):
                relay(m, j).wait_send()

        return 0

    lax.fori_loop(0, micros, close, 0)
    for kind in range(3):
        swap(kind).wait_send()
        for step in range(1, half):
            spread(kind, step).wait_send()


def local(
    sections, tiles,
    stored_inputs, cotangent, w_reduce, w_spatial, w_expand, bias_reduce, bias_spatial, bias_expand,
):
    _, micros, rows, cols, model = stored_inputs.shape
    bottle = w_reduce.shape[2]
    half = tiles // 2
    spans = (model // tiles, 9 * bottle // tiles, bottle // tiles)
    wides = (bottle, bottle, model)
    vmem = pltpu.VMEM
    dma = pltpu.SemaphoreType.DMA
    whole = pl.BlockSpec(memory_space=pltpu.VMEM)
    scratch = [
        vmem((micros, rows, cols, model), BF),
        vmem((micros, rows, cols, bottle), F32),
        vmem((micros, rows, cols, bottle), F32),
        vmem((micros, rows, cols, model), F32),
        vmem((micros, rows + 2, cols + 2 * PAD, bottle), F32),
        vmem((3, micros, rows + 2, cols, bottle), BF),
        vmem((micros, rows, cols, bottle), BF),
        vmem((micros, rows + 2, cols + 2 * PAD, bottle), F32),
        vmem((rows, cols, model), BF),
        vmem((rows, cols, bottle), BF),
    ]
    scratch += [vmem((bottle, model), BF), vmem((9 * bottle, bottle), BF), vmem((model, bottle), BF)]
    scratch += [vmem((micros, 2, cols, bottle), BF)] * 4
    scratch += [vmem((span * tiles, wide), F32) for span, wide in zip(spans, wides)]
    for count in (half, half, half, half - 1):
        scratch += [vmem((count, span, wide), BF) for span, wide in zip(spans, wides)]
    pieces = micros * PIECES
    scratch += [
        dma((micros,)), dma((pieces,)), dma((pieces,)), dma((micros, 2)), dma((micros, 2)),
        dma((pieces, 2)), dma((pieces, 2)), dma((3,)), dma((3,)), dma((3 * half,)), dma((3 * half,)),
    ]
    outs = pl.pallas_call(
        functools.partial(kernel, sections, tiles),
        out_shape=[jax.ShapeDtypeStruct((micros, rows, cols, model), BF)]
        + [jax.ShapeDtypeStruct((span, wide), F32) for span, wide in zip(spans, wides)],
        in_specs=[whole, pl.BlockSpec(memory_space=pl.ANY)] + [whole] * 6,
        out_specs=[whole] * 4,
        scratch_shapes=scratch,
        compiler_params=pltpu.CompilerParams(
            collective_id=0, has_side_effects=True, vmem_limit_bytes=66 * 1024 * 1000
        ),
    )(
        stored_inputs[0], cotangent, w_reduce[0], w_spatial[0], w_expand[0],
        bias_reduce, bias_spatial, bias_expand,
    )
    return tuple(out[None] for out in outs)


def solution(mesh):
    return jax.shard_map(
        functools.partial(local, mesh.shape["section"], mesh.shape["tile"]),
        mesh=mesh,
        in_specs=(
            P("section", None, "tile", None, None),
            P(None, "tile", None, None),
            P("section", None, None),
            P("section", None, None),
            P("section", None, None),
            P("section", None),
            P("section", None),
            P("section", None),
        ),
        out_specs=(
            P("section", None, "tile", None, None),
            P("section", "tile", None),
            P("section", "tile", None),
            P("section", "tile", None),
        ),
        check_vma=False,
    )
```

```python
import functools

import jax
import jax.numpy as jnp
from jax import lax
from jax.experimental import pallas as pl
from jax.experimental.pallas import tpu as pltpu
from jax.sharding import PartitionSpec as P

BF = jnp.bfloat16
F32 = jnp.float32
PAD = 8
PIECES = 8
LAG = 2
WIDE_OUTER = 4
WIDE_INNER = 2


def silu_and_slope(pre_act):
    sigma_val = jax.nn.sigmoid(pre_act)
    return pre_act * sigma_val, sigma_val * (1.0 + pre_act * (1.0 - sigma_val))


def dot_nn(left, right):
    return jnp.dot(left, right, preferred_element_type=F32)


def dot_tn(left, right):
    return lax.dot_general(left, right, (((0,), (0,)), ((), ())), preferred_element_type=F32)


def kernel(
    sections, tiles, x_ref, cot_ref, w1_ref, w2_ref, w3_ref, b1_ref, b2_ref, b3_ref,
    gin_ref, o1_ref, o2_ref, o3_ref,
    up, slope1, slope2, slope3, act_pad, taps, act2, g_pad, g3, g1,
    t1, t2, t3, fe_out, fe_in, be_out, be_in, sum1, sum2, sum3,
    p1, p2, p3, q1, q2, q3, r1, r2, r3, s1, s2, s3,
    cot_sem, up_ss, up_rs, fe_ss, fe_rs, be_ss, be_rs, a_ss, a_rs, z_ss, z_rs,
):
    micros, rows, cols, model = x_ref.shape
    bottle = w1_ref.shape[1]
    pixels = rows * cols
    width = cols // PIECES
    half = tiles // 2
    sec = lax.axis_index("section")
    tile = lax.axis_index("tile")
    core = lax.rem(tile, 2)
    zed = tile // 2
    is_last = sec == sections - 1
    has_above = tile > 0
    has_below = tile < tiles - 1
    partner = tile + 1 - 2 * core

    barrier = pltpu.get_barrier_semaphore()

    def greet(cond, target):
        @pl.when(cond)
        def _():
            pl.semaphore_signal(barrier, inc=1, device_id=target, device_id_type=pl.DeviceIdType.MESH)

    greet(has_above, {"tile": tile - 1})
    greet(has_below, {"tile": tile + 1})
    greet(sec > 0, {"section": sec - 1})
    greet(sec < sections - 1, {"section": sec + 1})
    for step in range(1, half):
        other = lax.rem(zed + step, half) * 2 + core
        pl.semaphore_signal(barrier, inc=1, device_id={"tile": other}, device_id_type=pl.DeviceIdType.MESH)

    def cot_copy(m):
        return pltpu.make_async_copy(cot_ref.at[m], up.at[m], cot_sem.at[m])

    @pl.when(is_last)
    def _():
        for m in range(micros):
            cot_copy(m).start()

    act_pad[...] = jnp.zeros(act_pad.shape, F32)
    g_pad[...] = jnp.zeros(g_pad.shape, F32)
    sum1[...] = jnp.zeros(sum1.shape, F32)
    sum2[...] = jnp.zeros(sum2.shape, F32)
    sum3[...] = jnp.zeros(sum3.shape, F32)

    def remote(src, dst, ss, rs, target):
        return pltpu.make_async_remote_copy(
            src_ref=src, dst_ref=dst, send_sem=ss, recv_sem=rs,
            device_id=target, device_id_type=pl.DeviceIdType.MESH,
        )

    def fe_up(m):
        return remote(fe_out.at[m, 0], fe_in.at[m, 1], fe_ss.at[m, 0], fe_rs.at[m, 1], {"tile": tile - 1})

    def fe_down(m):
        return remote(fe_out.at[m, 1], fe_in.at[m, 0], fe_ss.at[m, 1], fe_rs.at[m, 0], {"tile": tile + 1})

    def cut(j):
        return pl.ds(j * width, width)

    def be_up(m, j):
        n = m * PIECES + j
        return remote(
            be_out.at[m, 0, cut(j)], be_in.at[m, 1, cut(j)], be_ss.at[n, 0], be_rs.at[n, 1],
            {"tile": tile - 1},
        )

    def be_down(m, j):
        n = m * PIECES + j
        return remote(
            be_out.at[m, 1, cut(j)], be_in.at[m, 0, cut(j)], be_ss.at[n, 1], be_rs.at[n, 0],
            {"tile": tile + 1},
        )

    def relay(m, j):
        n = m * PIECES + j
        return remote(
            gin_ref.at[m, :, cut(j)], up.at[m, :, cut(j)], up_ss.at[n], up_rs.at[n],
            {"section": sec - 1},
        )

    def reduce_in(m, _):
        for y in range(rows):
            pre = dot_nn(x_ref[m, y], w1_ref[...]) + b1_ref[...]
            act, slope = silu_and_slope(pre)
            slope1[m, y] = slope
            act = act.astype(BF)
            act_pad[m, y + 1, pl.ds(PAD, cols)] = act.astype(F32)
            if y == 0:
                fe_out[m, 0] = act
            if y == rows - 1:
                fe_out[m, 1] = act
        return 0

    reduce_in(0, 0)

    greetings = (
        has_above.astype(jnp.int32) + has_below.astype(jnp.int32) + (sec > 0).astype(jnp.int32)
        + (sec < sections - 1).astype(jnp.int32) + (half - 1)
    )
    pl.semaphore_wait(barrier, greetings)

    def share_rims(m):
        @pl.when(has_above)
        def _():
            fe_up(m).start()

        @pl.when(has_below)
        def _():
            fe_down(m).start()

    def reduce_and_share(m, _):
        reduce_in(m, 0)
        share_rims(m)
        return 0

    share_rims(0)
    for n in range(model // bottle):
        lanes = pl.ds(n * bottle, bottle)
        t1[:, lanes] = w1_ref[lanes, :].astype(F32).T.astype(BF)
        t3[lanes, :] = w3_ref[:, lanes].astype(F32).T.astype(BF)
    for n in range(9):
        band = pl.ds(n * bottle, bottle)
        t2[band, :] = w2_ref[band, :].astype(F32).T.astype(BF)
    def expand_out(m, _):
        @pl.when(has_above)
        def _():
            fe_down(m).wait_recv()
            act_pad[m, 0, pl.ds(PAD, cols)] = fe_in[m, 0].astype(F32)

        @pl.when(has_below)
        def _():
            fe_up(m).wait_recv()
            act_pad[m, rows + 1, pl.ds(PAD, cols)] = fe_in[m, 1].astype(F32)

        for shift in range(3):
            for y in range(rows + 2):
                taps[shift, m, y] = act_pad[m, y, pl.ds(PAD - 1 + shift, cols)].astype(BF)
        for y in range(rows):
            patch = jnp.concatenate(
                [taps[dx, m, y + dy] for dy in range(3) for dx in range(3)], axis=-1
            )
            pre = dot_nn(patch, w2_ref[...]) + b2_ref[...]
            act, slope = silu_and_slope(pre)
            slope2[m, y] = slope
            act = act.astype(BF)
            act2[m, y] = act
            for n in range(model // bottle):
                lanes = pl.ds(n * bottle, bottle)
                pre = dot_nn(act, w3_ref[:, lanes]) + b3_ref[:, lanes] + x_ref[m, y, :, lanes].astype(F32)
                slope3[m, y, :, lanes] = silu_and_slope(pre)[1]
        return 0

    @pl.when(jnp.logical_not(is_last))
    def _():
        lax.fori_loop(1, micros, reduce_and_share, 0)
        lax.fori_loop(0, micros, expand_out, 0)

    def outer_part(m, j, count, awaited):
        broad = count * width
        here = pl.ds(j * width, broad)
        if awaited:
            relay(m, j).wait_recv()

        for y in range(rows):
            g3[y, here] = (up[m, y, here].astype(F32) * slope3[m, y, here]).astype(BF)
        back = dot_nn(g3[:, here].reshape(rows * broad, model), t3[...])
        g2 = (back.reshape(rows, broad, bottle) * slope2[m, :, here]).astype(BF)
        g_pad[m, pl.ds(1, rows), pl.ds(PAD + j * width, broad)] = g2.astype(F32)
        be_out[m, 0, here] = g2[0]
        be_out[m, 1, here] = g2[rows - 1]

        @pl.when(has_above)
        def _():
            for i in range(j, j + count):
                be_up(m, i).start()

        @pl.when(has_below)
        def _():
            for i in range(j, j + count):
                be_down(m, i).start()

    def take_rims(m, j):
        @pl.when(has_above)
        def _():
            be_down(m, j).wait_recv()
            g_pad[m, 0, pl.ds(PAD + j * width, width)] = be_in[m, 0, cut(j)].astype(F32)

        @pl.when(has_below)
        def _():
            be_up(m, j).wait_recv()
            g_pad[m, rows + 1, pl.ds(PAD + j * width, width)] = be_in[m, 1, cut(j)].astype(F32)

    def inner_part(m, j, count):
        broad = count * width
        here = pl.ds(j * width, broad)
        moved = [
            g_pad[m, :, pl.ds(PAD + 1 + j * width - dx, broad)].astype(BF) for dx in range(3)
        ]
        patch = jnp.concatenate(
            [
                moved[dx][2 - dy : 2 - dy + rows].reshape(rows * broad, bottle)
                for dy in range(3)
                for dx in range(3)
            ],
            axis=-1,
        )
        total = dot_nn(patch, t2[...])
        grad = (total.reshape(rows, broad, bottle) * slope1[m, :, here]).astype(BF)
        g1[:, here] = grad
        flat = grad.reshape(rows * broad, bottle)
        for n in range(model // bottle):
            lanes = pl.ds(n * bottle, bottle)
            back = dot_nn(flat, t1[:, lanes]).reshape(rows, broad, bottle)
            direct = up[m, :, here, lanes].astype(F32) * slope3[m, :, here, lanes]
            gin_ref[m, :, here, lanes] = (back + direct).astype(BF)

        @pl.when(sec > 0)
        def _():
            for i in range(j, j + count):
                relay(m, i).start()

    def outer_sums(m):
        sum3[...] += dot_tn(act2[m].reshape(pixels, bottle), g3[...].reshape(pixels, model))
        g2 = g_pad[m, pl.ds(1, rows), pl.ds(PAD, cols)].astype(BF).reshape(pixels, bottle)
        for dy in range(3):
            for dx in range(3):
                patch = taps[dx, m, pl.ds(dy, rows)].reshape(pixels, bottle)
                sum2[pl.ds((3 * dy + dx) * bottle, bottle)] += dot_tn(patch, g2)

    def backward(m, _):
        @pl.when(is_last)
        def _():
            expand_out(m, 0)
            cot_copy(m).wait()
            for j in range(0, PIECES, WIDE_OUTER):
                outer_part(m, j, WIDE_OUTER, False)

            @pl.when(m < micros - 1)
            def _():
                reduce_and_share(m + 1, 0)

            for j in range(PIECES):
                take_rims(m, j)
            for j in range(0, PIECES, WIDE_INNER):
                inner_part(m, j, WIDE_INNER)

        @pl.when(jnp.logical_not(is_last))
        def _():
            for j in range(PIECES):
                outer_part(m, j, 1, True)
                if j >= LAG:
                    take_rims(m, j - LAG)
                if j > LAG:
                    inner_part(m, j - LAG - 1, 1)
            for j in range(PIECES - LAG, PIECES):
                take_rims(m, j)
                inner_part(m, j - 1, 1)
            inner_part(m, PIECES - 1, 1)

        outer_sums(m)
        sum1[...] += dot_tn(x_ref[m].reshape(pixels, model), g1[...].reshape(pixels, bottle))
        return 0

    lax.fori_loop(0, micros, backward, 0)

    kinds = (
        (sum3, p3, q3, r3, s3, o3_ref),
        (sum2, p2, q2, r2, s2, o2_ref),
        (sum1, p1, q1, r1, s1, o1_ref),
    )

    def swap(kind):
        total, sent, got, _, _, _ = kinds[kind]
        return remote(sent, got, a_ss.at[kind], a_rs.at[kind], {"tile": partner})

    def spread(kind, step):
        _, _, _, part, landed, _ = kinds[kind]
        there = lax.rem(zed + step, half)
        n = kind * half + step
        return remote(
            part.at[there], landed.at[step - 1], z_ss.at[n], z_rs.at[n], {"tile": there * 2 + core}
        )

    for kind, (total, sent, _, _, _, out) in enumerate(kinds):
        span = out.shape[0]
        for z in range(half):
            first = pl.multiple_of((2 * z + 1 - core) * span, 16)
            sent[z] = total[pl.ds(first, span)].astype(BF)
        swap(kind).start()
    for kind, (total, _, got, part, _, out) in enumerate(kinds):
        span = out.shape[0]
        swap(kind).wait_recv()
        for z in range(half):
            first = pl.multiple_of((2 * z + core) * span, 16)
            part[z] = (total[pl.ds(first, span)] + got[z].astype(F32)).astype(BF)
        for step in range(1, half):
            spread(kind, step).start()
        own = pl.multiple_of((2 * zed + core) * span, 16)
        out[...] = total[pl.ds(own, span)] + got[zed].astype(F32)
    for kind, (_, _, _, _, landed, out) in enumerate(kinds):
        value = out[...]
        for step in range(1, half):
            spread(kind, step).wait_recv()
            value = value + landed[step - 1].astype(F32)
        out[...] = value

    def close(m, _):
        @pl.when(has_above)
        def _():
            fe_up(m).wait_send()
            for j in range(PIECES):
                be_up(m, j).wait_send()

        @pl.when(has_below)
        def _():
            fe_down(m).wait_send()
            for j in range(PIECES):
                be_down(m, j).wait_send()

        @pl.when(sec > 0)
        def _():
            for j in range(PIECES):
                relay(m, j).wait_send()

        return 0

    lax.fori_loop(0, micros, close, 0)
    for kind in range(3):
        swap(kind).wait_send()
        for step in range(1, half):
            spread(kind, step).wait_send()


def local(
    sections, tiles,
    stored_inputs, cotangent, w_reduce, w_spatial, w_expand, bias_reduce, bias_spatial, bias_expand,
):
    _, micros, rows, cols, model = stored_inputs.shape
    bottle = w_reduce.shape[2]
    half = tiles // 2
    spans = (model // tiles, 9 * bottle // tiles, bottle // tiles)
    wides = (bottle, bottle, model)
    vmem = pltpu.VMEM
    dma = pltpu.SemaphoreType.DMA
    whole = pl.BlockSpec(memory_space=pltpu.VMEM)
    scratch = [
        vmem((micros, rows, cols, model), BF),
        vmem((micros, rows, cols, bottle), F32),
        vmem((micros, rows, cols, bottle), F32),
        vmem((micros, rows, cols, model), F32),
        vmem((micros, rows + 2, cols + 2 * PAD, bottle), F32),
        vmem((3, micros, rows + 2, cols, bottle), BF),
        vmem((micros, rows, cols, bottle), BF),
        vmem((micros, rows + 2, cols + 2 * PAD, bottle), F32),
        vmem((rows, cols, model), BF),
        vmem((rows, cols, bottle), BF),
    ]
    scratch += [vmem((bottle, model), BF), vmem((9 * bottle, bottle), BF), vmem((model, bottle), BF)]
    scratch += [vmem((micros, 2, cols, bottle), BF)] * 4
    scratch += [vmem((span * tiles, wide), F32) for span, wide in zip(spans, wides)]
    for count in (half, half, half, half - 1):
        scratch += [vmem((count, span, wide), BF) for span, wide in zip(spans, wides)]
    pieces = micros * PIECES
    scratch += [
        dma((micros,)), dma((pieces,)), dma((pieces,)), dma((micros, 2)), dma((micros, 2)),
        dma((pieces, 2)), dma((pieces, 2)), dma((3,)), dma((3,)), dma((3 * half,)), dma((3 * half,)),
    ]
    outs = pl.pallas_call(
        functools.partial(kernel, sections, tiles),
        out_shape=[jax.ShapeDtypeStruct((micros, rows, cols, model), BF)]
        + [jax.ShapeDtypeStruct((span, wide), F32) for span, wide in zip(spans, wides)],
        in_specs=[whole, pl.BlockSpec(memory_space=pl.ANY)] + [whole] * 6,
        out_specs=[whole] * 4,
        scratch_shapes=scratch,
        compiler_params=pltpu.CompilerParams(
            collective_id=0, has_side_effects=True, vmem_limit_bytes=66 * 1024 * 1000
        ),
    )(
        stored_inputs[0], cotangent, w_reduce[0], w_spatial[0], w_expand[0],
        bias_reduce, bias_spatial, bias_expand,
    )
    return tuple(out[None] for out in outs)


def solution(mesh):
    return jax.shard_map(
        functools.partial(local, mesh.shape["section"], mesh.shape["tile"]),
        mesh=mesh,
        in_specs=(
            P("section", None, "tile", None, None),
            P(None, "tile", None, None),
            P("section", None, None),
            P("section", None, None),
            P("section", None, None),
            P("section", None),
            P("section", None),
            P("section", None),
        ),
        out_specs=(
            P("section", None, "tile", None, None),
            P("section", "tile", None),
            P("section", "tile", None),
            P("section", "tile", None),
        ),
        check_vma=False,
    )
```
